32 devices in a mesh: dp: 4 (over x, core), expert: 8 (over z, y).
Axes of the slice: x: 2, y: 2, z: 4, core: 2. Of those that a mesh axis runs over, the one named last changes fastest.
Arguments:
- tokens: bfloat16 [16384, 768], P(('dp', 'expert')), may hold values from -6 to 6
- routes: int32 [16384, 1], P(('dp', 'expert')), may hold values from 0 to 7; in each aligned block of 512 rows (0 to 511, 512 to 1023, ...) at most 80 rows name the same one
- domain_ids: int32 [32], replicated, may hold values from 0 to 7
- domain_weight: float32 [8], replicated, may hold values from 0.5 to 2
- qkv_weight: bfloat16 [2, 768, 2304], replicated, may hold values from -0.21875 to 0.21875
- out_weight: bfloat16 [2, 768, 768], replicated, may hold values from -0.625 to 0.625
- norm_gain: float32 [4, 768], replicated, may hold values from 0.5 to 1.5
- norm_shift: float32 [4, 768], replicated, may hold values from -2 to 2
- ffn_up: bfloat16 [768, 3072], replicated, may hold values from -0.21875 to 0.21875
- ffn_down: bfloat16 [3072, 768], replicated, may hold values from -0.109375 to 0.109375
- centroid: bfloat16 [8, 768], replicated, may hold values from -0.21875 to 0.21875
- expert_up: bfloat16 [8, 768, 3072], P('expert'), may hold values from -0.21875 to 0.21875
- expert_down: bfloat16 [8, 3072, 768], P('expert'), may hold values from -0.109375 to 0.109375
- cotangent: bfloat16 [16384, 768], P(('dp', 'expert')), may hold values from -6 to 6
Outputs:
- result: bfloat16 [16384, 768], P(('dp', 'expert'))
- tokens_grad: float32 [16384, 768], P(('dp', 'expert'))
- qkv_grad: float32 [2, 768, 2304], P(None, 'expert')
- out_grad: float32 [2, 768, 768], P(None, 'expert')
- gain_grad: float32 [4, 768], P(None, 'expert')
- shift_grad: float32 [4, 768], P(None, 'expert')
- up_grad: float32 [768, 3072], P(None, 'expert')
- down_grad: float32 [3072, 768], P(None, 'expert')
- centroid_grad: float32 [8, 768], P(None, 'expert')
- expert_up_grad: float32 [8, 768, 3072], P('expert', 'dp')
- expert_down_grad: float32 [8, 3072, 768], P('expert', 'dp')
The draws below stay inside these ranges and needn't reach their ends.
Inputs may be any that keep to these rules, and one draw needn't show every extreme that they name: `routes`: within the 512 tokens of one device no expert is named more than 80 times, a bound that some block reaches.
All inputs are finite; a program needn't handle non-finite values.
Results may differ from the reference program's by a relative error of at most 0.018.
Values may be sent and summed in bfloat16 or wider, within the bound.
No kernel may reach another device: no remote copies, remote signals or barrier semaphores. Data moves between devices by JAX's collectives and lax.ppermute only.
A program may use at most 256 MiB of HBM per device.

```python
import math
import jax
import jax.numpy as jnp
import numpy as np
from jax import lax

D = 768
HEADS = 12
HEAD_DIM = 64
FF = 3072
SEQ = 512
GROUPS = 8
EXPERTS = 8
CAP = 80
SEQS = 32
TOKENS = 16384


def with_ends(values, stream_key, smallest, high):
    longest = values.shape.index(max(values.shape))
    spots = []
    for shift in (0, 1):
        where = [jax.random.randint(jax.random.fold_in(stream_key, axis), (), 0, length) for axis, length in enumerate(values.shape)]
        where[longest] = (where[longest] + shift) % values.shape[longest]
        spots.append(tuple(where))
    return values.at[spots[0]].set(smallest).at[spots[1]].set(high)


def level_of(rng, dims, pieces, low, largest):
    loudness = 1.0
    for axis_at, parts in pieces:
        draws = jax.random.uniform(jax.random.fold_in(jax.random.fold_in(rng, 6), axis_at), (parts,), jnp.float32, low / len(pieces), largest / len(pieces))
        loudness = loudness * jnp.repeat(jnp.exp(draws), dims[axis_at] // parts).reshape((-1,) + (1,) * (len(dims) - 1 - axis_at))
    return loudness


def assign_block(own_key, own, number, rows, number_of, top, most, lean):
    sequence = jax.random.permutation(own_key, number_of)
    heavy_load, usual = load_shares(number_of, rows * top, most, lean, True), load_shares(number_of, rows * top, most, lean, False)
    places = jnp.arange(number_of)

    def named(sizes, rotation):
        used = int((sizes > 0).sum())
        fixed = max(1, used // 4)
        shifted = fixed + (places - fixed + rotation * (used - fixed)) % max(1, number_of - fixed)
        return jnp.zeros((number_of,), jnp.int32).at[sequence[jnp.where(places < fixed, places, shifted)]].set(jnp.asarray(sizes, jnp.int32))

    sizes = jnp.where(number % 4 == 0, named(heavy_load, number // 4), named(usual, number - number // 4 - 1))
    mixed = jax.random.permutation(jax.random.fold_in(own, 3), number_of)
    giver, receiver = mixed[0:number_of // 2 * 2:2], mixed[1:number_of // 2 * 2:2]
    slack = jnp.minimum(sizes[giver] - 1, most - sizes[receiver]) // 2
    slack = jnp.where((giver == sequence[0]) | (receiver == sequence[0]) | (sizes[receiver] == 0), 0, jnp.maximum(slack, 0))
    shifted = jax.random.randint(jax.random.fold_in(own, 4), (number_of // 2,), 0, 1 << 20) % (slack + 1)
    sizes = sizes.at[giver].add(-shifted).at[receiver].add(shifted)
    labels = jnp.searchsorted(jnp.cumsum(sizes), jnp.arange(rows * top), side="right").astype(jnp.int32)
    table = labels.reshape(top, rows).T
    table = table[jax.random.permutation(jax.random.fold_in(own, 1), rows)]
    rotation = jax.random.randint(jax.random.fold_in(own, 2), (rows, 1), 0, top)
    return jnp.take_along_axis(table, (jnp.arange(top)[None, :] + rotation) % top, axis=1)


def load_shares(number_of, total, limit, lean, full):
    weights = [(1 << 20) // math.isqrt(standing ** lean) + 1 for standing in range(1, number_of + 1)]
    largest = limit if full else min(limit, max(-(-total // number_of), total * weights[0] // sum(weights)))
    least = 1 if total - largest >= number_of - 1 else 0
    given, spare = [largest] + [least] * (number_of - 1), total - largest - least * (number_of - 1)
    while spare > 0:
        candidates = [i for i in range(1, number_of) if given[i] < largest] or [i for i in range(1, number_of) if given[i] < limit]
        mass, remaining = sum([weights[i] for i in candidates]), spare
        for i in candidates:
            extra = min(limit - given[i], max(1, remaining * weights[i] // mass), spare)
            given[i] = given[i] + extra
            spare = spare - extra
    return np.array(given)


def bell_draw(stream_key, dims, width, bound, split=(), kind=jnp.bfloat16):
    values = width * jax.random.normal(stream_key, dims, jnp.float32)
    if split:
        values = values * level_of(stream_key, dims, split, -0.22, 0.18)
    return jnp.clip(values, -bound, bound).astype(kind)


def setup_inputs(seed: int = 0) -> dict:
    seeds = jax.random.split(jax.random.key(seed), 15)
    tokens = bell_draw(seeds[0], (TOKENS, D), 1.0, 6.0, ((0, 32),))
    routes_keys = jax.random.split(jax.random.fold_in(seeds[1], 1), TOKENS // SEQ)
    routes_turns = jax.random.permutation(jax.random.fold_in(seeds[1], 3), TOKENS // SEQ)
    routes = jax.vmap(lambda own, number: assign_block(jax.random.fold_in(seeds[1], 2), own, number, SEQ, EXPERTS, 1, CAP, 1))(routes_keys, routes_turns).reshape((TOKENS, 1))
    domain_ids = with_ends(jax.random.randint(seeds[2], (SEQS,), 0, GROUPS), jax.random.fold_in(seeds[2], 1), 0, GROUPS - 1).astype(jnp.int32)
    domain_weight = jnp.clip(jnp.exp(jax.random.uniform(seeds[3], (GROUPS,), jnp.float32, math.log(0.5), math.log(2.0))), 0.5, 2.0)
    qkv_weight = bell_draw(seeds[4], (2, D, 3 * D), D ** -0.5, 0.21875)
    out_weight = bell_draw(seeds[5], (2, D, D), (D // 8) ** -0.5, 0.625)
    norm_gain = jnp.clip(1.0 + 0.1 * jax.random.normal(seeds[6], (4, D), jnp.float32), 0.5, 1.5)
    norm_shift = bell_draw(seeds[7], (4, D), 0.3, 2.0, (), jnp.float32)
    ffn_up = bell_draw(seeds[8], (D, FF), D ** -0.5, 0.21875)
    ffn_down = bell_draw(seeds[9], (FF, D), FF ** -0.5, 0.109375)
    centroid = bell_draw(seeds[10], (EXPERTS, D), D ** -0.5, 0.21875)
    expert_up = bell_draw(seeds[11], (EXPERTS, D, FF), D ** -0.5, 0.21875, ((0, 8),))
    expert_down = bell_draw(seeds[12], (EXPERTS, FF, D), FF ** -0.5, 0.109375, ((0, 8),))
    cotangent = bell_draw(seeds[13], (TOKENS, D), 1.0, 6.0, ((0, 32),))
    return {"tokens": tokens, "routes": routes, "domain_ids": domain_ids, "domain_weight": domain_weight, "qkv_weight": qkv_weight, "out_weight": out_weight, "norm_gain": norm_gain, "norm_shift": norm_shift, "ffn_up": ffn_up, "ffn_down": ffn_down, "centroid": centroid, "expert_up": expert_up, "expert_down": expert_down, "cotangent": cotangent}


highest = lax.Precision.HIGHEST

@jax.custom_vjp
def low(v):
    return lax.optimization_barrier(v.astype(jnp.bfloat16)).astype(jnp.float32)

@jax.custom_vjp
def low_back(v):
    return v

def low_keep(v):
    return (low(v), None)

def low_pass(kept, grad):
    return (grad,)

def back_keep(v):
    return (v, None)

def back_low(kept, grad):
    return (low(grad),)
low.defvjp(low_keep, low_pass)
low_back.defvjp(back_keep, back_low)

def matmul(left_side, right_side):
    return jnp.dot(left_side, right_side, precision=highest, preferred_element_type=jnp.float32)

def gelu_exact(activation):
    return jax.nn.gelu(activation, approximate=False)

def layer_norm(activation, gain_row, shift_row):
    center = activation - lax.optimization_barrier(jnp.mean(activation, axis=-1, keepdims=True))
    spread = lax.optimization_barrier(jnp.mean(center * center, axis=-1, keepdims=True))
    return center * lax.rsqrt(spread + 1e-05) * gain_row + shift_row

def attend(hidden, qkv_matrix, out_matrix, gain_row, shift_row):
    length = hidden.shape[0]
    normed = low(layer_norm(hidden, gain_row, shift_row))
    packed = low(low_back(matmul(normed, qkv_matrix)))
    query_rows = packed[:, :D].reshape(length, HEADS, HEAD_DIM)
    key_rows = packed[:, D:2 * D].reshape(length, HEADS, HEAD_DIM)
    value_rows = packed[:, 2 * D:].reshape(length, HEADS, HEAD_DIM)
    scores = jnp.einsum('qhd,khd->hqk', query_rows, key_rows, precision=highest) * (1.0 / math.sqrt(HEAD_DIM))
    scores = low_back(scores)
    position = jnp.arange(length)
    causal = position[None, :] <= position[:, None]
    scores = jnp.where(causal[None], scores, -1e+30)
    weights = low(jax.nn.softmax(scores, axis=-1))
    attended = jnp.einsum('hqk,khd->qhd', weights, value_rows, precision=highest).reshape(length, D)
    attended = low(low_back(attended))
    return low_back(matmul(attended, out_matrix))

def feed_forward(hidden, up_matrix, down_matrix, gain_row, shift_row):
    normed = low(layer_norm(hidden, gain_row, shift_row))
    pre_act = low_back(matmul(normed, up_matrix))
    activated = low(gelu_exact(pre_act))
    return low_back(matmul(activated, down_matrix))

def mixture(hidden, route_row, centroid_rows, up_stack, down_stack, gain_row, shift_row):
    normed = low(layer_norm(hidden, gain_row, shift_row))
    chosen = centroid_rows[route_row]
    gate_value = jax.nn.sigmoid(lax.optimization_barrier(jnp.sum(normed * chosen, axis=-1)))
    one_hot = (route_row[:, None] == jnp.arange(EXPERTS)[None, :]).astype(jnp.int32)
    slot_ranks = lax.optimization_barrier(jnp.sum((jnp.cumsum(one_hot, axis=0) - one_hot) * one_hot, axis=1))
    slot_index = (route_row * CAP + slot_ranks).astype(jnp.int32)
    inputs = low_back(normed)
    buffer_rows = jnp.zeros((EXPERTS * CAP, D), jnp.float32).at[slot_index].set(inputs)
    buffer_rows = buffer_rows.reshape(EXPERTS, CAP, D)
    pre_act = low_back(jnp.einsum('ecd,edf->ecf', buffer_rows, up_stack, precision=highest))
    activated = low(gelu_exact(pre_act))
    expert_out = low(low_back(jnp.einsum('ecf,efd->ecd', activated, down_stack, precision=highest)))
    picked = expert_out.reshape(EXPERTS * CAP, D)[slot_index]
    return gate_value[:, None] * picked

def forward(hidden, route_row, qkv_all, out_all, gains, shifts, up_matrix, down_matrix, centroid_rows, up_stack, down_stack):
    hidden = hidden + attend(hidden, qkv_all[0], out_all[0], gains[0], shifts[0])
    hidden = hidden + feed_forward(hidden, up_matrix, down_matrix, gains[1], shifts[1])
    hidden = hidden + attend(hidden, qkv_all[1], out_all[1], gains[2], shifts[2])
    return hidden + mixture(hidden, route_row, centroid_rows, up_stack, down_stack, gains[3], shifts[3])

def reference(tokens, routes, domain_ids, domain_weight, qkv_weight, out_weight, norm_gain, norm_shift, ffn_up, ffn_down, centroid, expert_up, expert_down, cotangent):
    float_weights = (qkv_weight.astype(jnp.float32), out_weight.astype(jnp.float32), norm_gain.astype(jnp.float32), norm_shift.astype(jnp.float32), ffn_up.astype(jnp.float32), ffn_down.astype(jnp.float32), centroid.astype(jnp.float32), expert_up.astype(jnp.float32), expert_down.astype(jnp.float32))
    member = (domain_ids[:, None] == jnp.arange(GROUPS)[None, :]).astype(jnp.float32)
    counts = lax.optimization_barrier(jnp.sum(member, axis=0))
    seq_weight = domain_weight[domain_ids] * (SEQS / GROUPS) / counts[domain_ids]
    inputs = tokens.astype(jnp.float32).reshape(SEQS, SEQ, D)
    route_rows = routes.reshape(SEQS, SEQ).astype(jnp.int32)
    seed_rows = cotangent.astype(jnp.float32).reshape(SEQS, SEQ, D) * seq_weight[:, None, None]

    def one_sequence(running, pieces_in):
        hidden, route_row, seed_grad = pieces_in
        result, pullback = jax.vjp(lambda value_in, *weight_list: forward(value_in, route_row, *weight_list), hidden, *float_weights)
        gradients = pullback(seed_grad)
        running = tuple((total_now + fresh for total_now, fresh in zip(running, gradients[1:])))
        return (running, (result.astype(jnp.bfloat16), gradients[0]))
    zero_grads = tuple((jnp.zeros(weight_now.shape, jnp.float32) for weight_now in float_weights))
    totals, (results, input_grads) = lax.scan(one_sequence, zero_grads, (inputs, route_rows, seed_rows))
    return (results.reshape(TOKENS, D), input_grads.reshape(TOKENS, D), totals[0], totals[1], totals[2], totals[3], totals[4], totals[5], totals[6], totals[7], totals[8])
```

```python
import math

import jax
import jax.numpy as jnp
from jax import lax
from jax.sharding import PartitionSpec as P

HEADS = 12
HEAD_DIM = 64


highest = lax.Precision.HIGHEST
bf16 = jnp.bfloat16
f32 = jnp.float32


def bits_of(axis):
    size = lax.axis_size(axis)
    return [(axis, 1 << b) for b in range(size.bit_length() - 1)]


def swap(value, stage):
    axis, mask = stage
    size = lax.axis_size(axis)
    return lax.ppermute(value, axis, [(i, i ^ mask) for i in range(size)])


def my_bit(stage):
    axis, mask = stage
    return (lax.axis_index(axis) // mask) % 2


def round_bf16(value):
    return lax.reduce_precision(value.astype(f32), 8, 7)


def order_of(width, stages, use_expert=True):
    parts = 1 << len(stages)
    rest = width // parts
    row = jnp.arange(width, dtype=jnp.int32)
    inner = row % rest
    code = row // rest
    dp_bits = [s for s in stages if s[0] == "dp"]
    expert = jnp.zeros_like(row)
    piece = jnp.zeros_like(row)
    for at, stage in enumerate(stages):
        bit = ((code >> (len(stages) - 1 - at)) & 1) ^ my_bit(stage).astype(jnp.int32)
        if stage[0] == "expert":
            expert = expert + bit * stage[1]
        else:
            piece = piece + bit * (1 << dp_bits.index(stage))
    return (expert * (1 << len(dp_bits)) + piece) * rest + inner


def reorder_columns(value, stages):
    width = value.shape[1]
    order = order_of(width, stages)
    pick = (jnp.arange(width, dtype=jnp.int32)[:, None] == order[None, :]).astype(bf16)
    return jnp.dot(value, pick, preferred_element_type=bf16)


def reorder_blocks(value, stages):
    parts = 1 << len(stages)
    size = value.shape[1] // parts
    order = order_of(parts, stages)
    return [lax.dynamic_slice_in_dim(value, order[i] * size, size, axis=1) for i in range(parts)]


def outer(left, right):
    return jnp.einsum("sd,se->de", left, right, preferred_element_type=f32).astype(bf16)


def outer_halves(left, right, stages):
    ordered = reorder_columns(left, stages)
    half = ordered.shape[1] // 2
    return (outer(ordered[:, :half], right), outer(ordered[:, half:], right))


def reduce_halves(kept, sent, stages):
    current = (kept.astype(f32) + swap(sent, stages[0]).astype(f32)).astype(bf16)
    for stage in stages[1:]:
        half = current.shape[0] // 2
        got = swap(current[half:], stage)
        current = (current[:half].astype(f32) + got.astype(f32)).astype(bf16)
    return current


def share_rows(current, all_stages, gather_stages):
    for stage in all_stages:
        mine = round_bf16(current)
        got = swap(mine.astype(bf16), stage)
        current = (mine + got.astype(f32)).astype(bf16)
    current = round_bf16(current).astype(bf16)[None]
    for stage in gather_stages:
        current = jnp.concatenate([current, swap(current, stage)], axis=0)
    mine = jnp.int32(0)
    for at, stage in enumerate(gather_stages):
        mine = mine + my_bit(stage).astype(jnp.int32) * (1 << at)
    rows = [
        lax.dynamic_index_in_dim(current, i ^ mine, 0, keepdims=False)
        for i in range(current.shape[0])
    ]
    return jnp.concatenate(rows, axis=0).astype(f32)

def gelu_exact(activation):
    return jax.nn.gelu(activation, approximate=False)


def layer_norm(activation, gain_row, shift_row):
    center = activation - jnp.mean(activation, axis=-1, keepdims=True)
    spread = jnp.mean(center * center, axis=-1, keepdims=True)
    return center * lax.rsqrt(spread + 1e-05) * gain_row + shift_row


def split_heads(packed, model_width):
    length = packed.shape[0]
    query_rows = packed[:, :model_width].reshape(length, HEADS, HEAD_DIM)
    key_rows = packed[:, model_width : 2 * model_width].reshape(length, HEADS, HEAD_DIM)
    value_rows = packed[:, 2 * model_width :].reshape(length, HEADS, HEAD_DIM)
    return (query_rows, key_rows, value_rows)


def block_scores(query_block, key_block):
    scores = jnp.einsum(
        "qhd,khd->hqk", query_block, key_block, preferred_element_type=jnp.float32
    ) * (1.0 / math.sqrt(HEAD_DIM))
    query_count = query_block.shape[0]
    key_count = key_block.shape[0]
    causal = jnp.arange(key_count)[None, :] <= jnp.arange(query_count)[:, None]
    return jnp.where(causal[None], scores, -1e30)


def attend_forward(hidden, qkv_matrix, out_matrix, gain_row, shift_row):
    length, model_width = hidden.shape
    normed = layer_norm(hidden, gain_row, shift_row).astype(jnp.bfloat16)
    packed = jnp.dot(normed, qkv_matrix, preferred_element_type=jnp.float32).astype(jnp.bfloat16)
    query_rows, key_rows, value_rows = split_heads(packed, model_width)
    scores = block_scores(query_rows, key_rows)
    logsum = jax.nn.logsumexp(scores, axis=-1, keepdims=True)
    weights = jnp.exp(scores - logsum).astype(jnp.bfloat16)
    pieces = jnp.einsum("hqk,khd->qhd", weights, value_rows, preferred_element_type=jnp.float32)
    attended = pieces.reshape(length, model_width).astype(jnp.bfloat16)
    branch = jnp.dot(attended, out_matrix, preferred_element_type=jnp.float32)
    return ((normed, packed, logsum, attended), branch)


def attend_backward(hidden, saved, grad_out, qkv_matrix, out_matrix, gain_row, shift_row):
    normed, packed, logsum_all, attended = saved
    length, model_width = hidden.shape
    score_scale = 1.0 / math.sqrt(HEAD_DIM)
    grad_branch = grad_out.astype(jnp.bfloat16)
    grad_attended = jnp.einsum(
        "se,de->sd", grad_branch, out_matrix, preferred_element_type=jnp.float32
    )
    grad_attended = grad_attended.astype(jnp.bfloat16).reshape(length, HEADS, HEAD_DIM)
    query_rows, key_rows, value_rows = split_heads(packed, model_width)
    block_rows = min(512, length)
    grad_key = jnp.zeros((length, HEADS, HEAD_DIM), jnp.float32)
    grad_value = jnp.zeros((length, HEADS, HEAD_DIM), jnp.float32)
    scores = block_scores(query_rows, key_rows)
    soft_probs = jnp.exp(scores - logsum_all)
    grad_probs = jnp.einsum(
        "qhd,khd->hqk", grad_attended, value_rows, preferred_element_type=jnp.float32
    )
    inner_sum = jnp.sum(grad_probs * soft_probs, axis=-1, keepdims=True)
    grad_scores = (soft_probs * (grad_probs - inner_sum)).astype(jnp.bfloat16)
    grad_value = grad_value.at[:block_rows].add(
        jnp.einsum(
            "hqk,qhd->khd",
            soft_probs.astype(jnp.bfloat16),
            grad_attended,
            preferred_element_type=jnp.float32,
        )
    )
    grad_key = grad_key.at[:block_rows].add(
        jnp.einsum("hqk,qhd->khd", grad_scores, query_rows, preferred_element_type=jnp.float32)
        * score_scale
    )
    grad_query = (
        jnp.einsum("hqk,khd->qhd", grad_scores, key_rows, preferred_element_type=jnp.float32)
        * score_scale
    )
    grad_packed = jnp.concatenate(
        [
            grad_query.reshape(length, model_width),
            grad_key.reshape(length, model_width),
            grad_value.reshape(length, model_width),
        ],
        axis=1,
    ).astype(jnp.bfloat16)
    grad_normed = jnp.einsum(
        "se,de->sd", grad_packed, qkv_matrix, preferred_element_type=jnp.float32
    )
    ignored, pullback = jax.vjp(layer_norm, hidden, gain_row, shift_row)
    grad_hidden, gain_part, shift_part = pullback(grad_normed)
    return (grad_hidden, grad_packed, grad_branch, gain_part, shift_part)


def ffn_forward(hidden, up_matrix, down_matrix, gain_row, shift_row):
    normed = layer_norm(hidden, gain_row, shift_row).astype(jnp.bfloat16)
    pre_act = jnp.dot(normed, up_matrix, preferred_element_type=jnp.float32)
    activated = gelu_exact(pre_act).astype(jnp.bfloat16)
    return (
        (normed, pre_act, activated),
        jnp.dot(activated, down_matrix, preferred_element_type=jnp.float32),
    )


def ffn_backward(hidden, saved, grad_out, up_matrix, down_matrix, gain_row, shift_row):
    normed, pre_act, activated = saved
    grad_branch = grad_out.astype(jnp.bfloat16)
    grad_activated = jnp.einsum(
        "sd,fd->sf", grad_branch, down_matrix, preferred_element_type=jnp.float32
    )
    ignored, pullback = jax.vjp(gelu_exact, pre_act)
    grad_pre = pullback(grad_activated)[0].astype(jnp.bfloat16)
    grad_normed = jnp.einsum("sf,df->sd", grad_pre, up_matrix, preferred_element_type=jnp.float32)
    ignored_too, norm_pullback = jax.vjp(layer_norm, hidden, gain_row, shift_row)
    grad_hidden, gain_part, shift_part = norm_pullback(grad_normed)
    return (grad_hidden, grad_pre, grad_branch, gain_part, shift_part)


def local(
    tokens,
    routes,
    domain_ids,
    domain_weight,
    qkv_weight,
    out_weight,
    norm_gain,
    norm_shift,
    ffn_up,
    ffn_down,
    centroid,
    expert_up,
    expert_down,
    cotangent,
):
    length, model_width = tokens.shape
    experts = centroid.shape[0]
    capacity = 5 * length // (4 * experts)
    groups = domain_weight.shape[0]
    sequences = domain_ids.shape[0]
    position = lax.axis_index("dp") * lax.axis_size("expert") + lax.axis_index("expert")
    member = (domain_ids[:, None] == jnp.arange(groups)[None, :]).astype(jnp.float32)
    counts = jnp.sum(member, axis=0)
    own_group = lax.dynamic_index_in_dim(member, position, 0, keepdims=False)
    seq_weight = (
        jnp.sum(own_group * domain_weight) * (sequences / groups) / jnp.sum(own_group * counts)
    )
    hidden0 = tokens.astype(jnp.float32)
    saved0, branch0 = attend_forward(
        hidden0, qkv_weight[0], out_weight[0], norm_gain[0], norm_shift[0]
    )
    hidden1 = hidden0 + branch0
    saved_ffn, branch_ffn = ffn_forward(hidden1, ffn_up, ffn_down, norm_gain[1], norm_shift[1])
    hidden2 = hidden1 + branch_ffn
    saved1, branch1 = attend_forward(
        hidden2, qkv_weight[1], out_weight[1], norm_gain[2], norm_shift[2]
    )
    hidden3 = hidden2 + branch1
    normed = layer_norm(hidden3, norm_gain[3], norm_shift[3]).astype(jnp.bfloat16)
    normed_f = normed.astype(jnp.float32)
    route_row = routes[:, 0]
    one_hot = (route_row[:, None] == jnp.arange(experts)[None, :]).astype(jnp.int32)
    slot_ranks = jnp.sum((jnp.cumsum(one_hot, axis=0) - one_hot) * one_hot, axis=1)
    slot_index = route_row * capacity + slot_ranks
    selector = one_hot.astype(bf16)
    chosen = jnp.dot(selector, centroid, preferred_element_type=f32)
    gate_logit = jnp.sum(normed_f * chosen, axis=-1)
    gate_value = jax.nn.sigmoid(gate_logit)
    slots = experts * capacity
    place = (jnp.arange(slots, dtype=jnp.int32)[:, None] == slot_index[None, :]).astype(bf16)

    def to_slots(rows):
        table = jnp.dot(place, rows, preferred_element_type=bf16)
        table = table.reshape(experts, capacity, model_width)
        return lax.all_to_all(table, "expert", split_axis=0, concat_axis=0, tiled=True)

    def from_slots(rows):
        table = rows.reshape(experts, capacity, model_width)
        back = lax.all_to_all(table, "expert", split_axis=0, concat_axis=0, tiled=True)
        back = back.reshape(slots, model_width)
        return jnp.einsum("ps,pd->sd", place, back, preferred_element_type=f32)

    slot_in = to_slots(normed).reshape(slots, model_width)
    seed_grad = cotangent.astype(f32) * seq_weight
    dslot_out = to_slots((gate_value[:, None] * seed_grad).astype(bf16)).reshape(slots, model_width)
    up_matrix = expert_up[0]
    down_matrix = expert_down[0]
    pre_act = jnp.dot(slot_in, up_matrix, preferred_element_type=f32)
    eact = gelu_exact(pre_act).astype(bf16)
    eout = jnp.dot(eact, down_matrix, preferred_element_type=f32).astype(bf16)
    picked = from_slots(eout)
    grad_eact = jnp.einsum("sd,fd->sf", dslot_out, down_matrix, preferred_element_type=f32)
    ignored_gelu, gelu_pullback = jax.vjp(gelu_exact, pre_act)
    grad_epre = gelu_pullback(grad_eact)[0].astype(bf16)
    dslot_in = jnp.einsum("sf,df->sd", grad_epre, up_matrix, preferred_element_type=f32).astype(bf16)
    returned_grads = from_slots(dslot_in)

    dp_stages = bits_of("dp")
    core = dp_stages[0]
    expert_stages = bits_of("expert")
    expert_first = [core] + expert_stages
    dp_first = dp_stages + expert_stages

    up_kept, up_sent = outer_halves(slot_in, grad_epre, dp_stages)
    eact_blocks = reorder_blocks(eact, dp_stages)
    half = len(eact_blocks) // 2
    down_kept = jnp.concatenate([outer(block, dslot_out) for block in eact_blocks[:half]], axis=0)
    down_sent = jnp.concatenate([outer(block, dslot_out) for block in eact_blocks[half:]], axis=0)
    expert_up_grad = reduce_halves(up_kept, up_sent, dp_stages).astype(f32)[None]
    expert_down_grad = reduce_halves(down_kept, down_sent, dp_stages).astype(f32)[None]

    result = (hidden3 + gate_value[:, None] * picked).astype(bf16)
    grad_gate = jnp.sum(seed_grad * picked, axis=-1)
    grad_logit = grad_gate * (gate_value * (1.0 - gate_value))
    centroid_part = jnp.einsum(
        "se,sd->ed",
        selector.astype(f32),
        grad_logit[:, None] * normed_f,
        precision=highest,
        preferred_element_type=f32,
    )
    grad_normed = grad_logit[:, None] * chosen + returned_grads
    ignored_norm, norm_pullback = jax.vjp(layer_norm, hidden3, norm_gain[3], norm_shift[3])
    grad_hidden, gain_norm3, shift_norm3 = norm_pullback(grad_normed)
    grad_h3 = seed_grad + grad_hidden

    def attention_pieces(saved, grad_packed, grad_branch, stages):
        qkv_kept, qkv_sent = outer_halves(saved[0], grad_packed, stages)
        out_kept, out_sent = outer_halves(saved[3], grad_branch, stages)
        return reduce_halves(
            jnp.concatenate([qkv_kept, out_kept], axis=1),
            jnp.concatenate([qkv_sent, out_sent], axis=1),
            stages,
        )

    grad_hidden, packed_late, branch_late, gain_norm2, shift_norm2 = attend_backward(
        hidden2, saved1, grad_h3, qkv_weight[1], out_weight[1], norm_gain[2], norm_shift[2]
    )
    late = attention_pieces(saved1, packed_late, branch_late, expert_first)
    late = share_rows(late, dp_stages[1:], dp_stages[:1])
    grad_h2 = grad_h3 + grad_hidden
    grad_hidden, grad_pre, branch_ffn_grad, gain_norm1, shift_norm1 = ffn_backward(
        hidden1, saved_ffn, grad_h2, ffn_up, ffn_down, norm_gain[1], norm_shift[1]
    )
    grad_h1 = grad_h2 + grad_hidden
    down_kept, down_sent = outer_halves(branch_ffn_grad, saved_ffn[2], dp_first)
    down_rows = share_rows(reduce_halves(down_kept, down_sent, dp_first), [], dp_stages)
    pre_blocks = jnp.stack(reorder_blocks(grad_pre, expert_stages))
    ordered = reorder_columns(saved_ffn[0], [core])
    half = ordered.shape[1] // 2

    def up_outer(left):
        made = jnp.einsum("sd,esf->edf", left, pre_blocks, preferred_element_type=f32)
        return made.astype(bf16).reshape(-1, made.shape[2])

    up_rows = reduce_halves(up_outer(ordered[:, :half]), up_outer(ordered[:, half:]), expert_first)
    up_rows = share_rows(up_rows, dp_stages[1:], dp_stages[:1])

    grad_hidden, packed_early, branch_early, gain_norm0, shift_norm0 = attend_backward(
        hidden0, saved0, grad_h1, qkv_weight[0], out_weight[0], norm_gain[0], norm_shift[0]
    )
    tokens_grad = grad_h1 + grad_hidden
    qk_width = 2 * model_width
    qk_kept, qk_sent = outer_halves(saved0[0], packed_early[:, :qk_width], dp_first)
    qk_rows = share_rows(reduce_halves(qk_kept, qk_sent, dp_first), [], dp_stages)
    v_kept, v_sent = outer_halves(saved0[0], packed_early[:, qk_width:], expert_first)
    out_kept, out_sent = outer_halves(saved0[3], branch_early, expert_first)
    vo_rows = reduce_halves(
        jnp.concatenate([v_kept, out_kept], axis=1),
        jnp.concatenate([v_sent, out_sent], axis=1),
        expert_first,
    )
    vo_rows = share_rows(vo_rows, dp_stages[1:], dp_stages[:1])
    small = jnp.concatenate(
        [
            jnp.stack([gain_norm0, gain_norm1, gain_norm2, gain_norm3]),
            jnp.stack([shift_norm0, shift_norm1, shift_norm2, shift_norm3]),
            centroid_part,
        ],
        axis=0,
    )
    small = lax.psum(small, ("dp", "expert"))
    own = model_width // experts
    small = lax.dynamic_slice_in_dim(small, lax.axis_index("expert") * own, own, axis=1)
    qkv_width = 3 * model_width
    return (
        result,
        tokens_grad,
        jnp.stack(
            [
                jnp.concatenate([qk_rows, vo_rows[:, :model_width]], axis=1),
                late[:, :qkv_width],
            ]
        ),
        jnp.stack([vo_rows[:, model_width:], late[:, qkv_width:]]),
        small[:4],
        small[4:8],
        up_rows,
        down_rows.T,
        small[8:],
        expert_up_grad,
        expert_down_grad,
    )


def solution(mesh):
    placed = (
        P(("dp", "expert"), None),
        P(("dp", "expert"), None),
        P(),
        P(),
        P(),
        P(),
        P(),
        P(),
        P(),
        P(),
        P(),
        P("expert", None, None),
        P("expert", None, None),
        P(("dp", "expert"), None),
    )
    return jax.shard_map(
        local,
        mesh=mesh,
        in_specs=placed,
        out_specs=(
            P(("dp", "expert"), None),
            P(("dp", "expert"), None),
            P(None, "expert", None),
            P(None, "expert", None),
            P(None, "expert"),
            P(None, "expert"),
            P(None, "expert"),
            P(None, "expert"),
            P(None, "expert"),
            P("expert", "dp", None),
            P("expert", "dp", None),
        ),
        check_vma=False,
    )
```

```python
import functools
import math

import jax
import jax.numpy as jnp
from jax import lax
from jax.experimental import pallas as pl
from jax.sharding import PartitionSpec as P

HEADS = 12
HEAD_DIM = 64
SCALE = HEAD_DIM**-0.5
LANES = 128


highest = lax.Precision.HIGHEST
bf16 = jnp.bfloat16
f32 = jnp.float32
PARTS = 1


def bits_of(axis):
    size = lax.axis_size(axis)
    return [(axis, 1 << b) for b in range(size.bit_length() - 1)]


def swap(value, stage):
    axis, mask = stage
    size = lax.axis_size(axis)
    return lax.ppermute(value, axis, [(i, i ^ mask) for i in range(size)])


def my_bit(stage):
    axis, mask = stage
    return (lax.axis_index(axis) // mask) % 2


def round_bf16(value):
    return lax.reduce_precision(value.astype(f32), 8, 7)


def order_of(width, stages, use_expert=True):
    parts = 1 << len(stages)
    rest = width // parts
    row = jnp.arange(width, dtype=jnp.int32)
    inner = row % rest
    code = row // rest
    dp_bits = [s for s in stages if s[0] == "dp"]
    expert = jnp.zeros_like(row)
    piece = jnp.zeros_like(row)
    for at, stage in enumerate(stages):
        bit = ((code >> (len(stages) - 1 - at)) & 1) ^ my_bit(stage).astype(jnp.int32)
        if stage[0] == "expert":
            expert = expert + bit * stage[1]
        else:
            piece = piece + bit * (1 << dp_bits.index(stage))
    return (expert * (1 << len(dp_bits)) + piece) * rest + inner


def reorder_columns(value, stages):
    width = value.shape[1]
    order = order_of(width, stages)
    pick = (jnp.arange(width, dtype=jnp.int32)[:, None] == order[None, :]).astype(bf16)
    return jnp.dot(value, pick, preferred_element_type=bf16)


def reorder_blocks(value, stages):
    parts = 1 << len(stages)
    size = value.shape[1] // parts
    order = order_of(parts, stages)
    return [lax.dynamic_slice_in_dim(value, order[i] * size, size, axis=1) for i in range(parts)]


def outer(left, right):
    return jnp.einsum("sd,se->de", left, right, preferred_element_type=f32).astype(bf16)


def outer_halves(left, right, stages):
    ordered = reorder_columns(left, stages)
    half = ordered.shape[1] // 2
    return (outer(ordered[:, :half], right), outer(ordered[:, half:], right))


def layer_norm(activation, gain_row, shift_row):
    center = activation - jnp.mean(activation, axis=-1, keepdims=True)
    spread = jnp.mean(center * center, axis=-1, keepdims=True)
    return center * lax.rsqrt(spread + 1e-05) * gain_row + shift_row


NT = (((1,), (1,)), ((), ()))


def dot_nt(left, right):
    return lax.dot_general(left, right, NT, preferred_element_type=f32)


def dot_nn(left, right):
    return jnp.dot(left, right, preferred_element_type=f32)


def causal_mask(rows):
    key = lax.broadcasted_iota(jnp.int32, (rows, rows), 0)
    query = lax.broadcasted_iota(jnp.int32, (rows, rows), 1)
    return key <= query


def attend_forward_kernel(q_ref, k_ref, v_ref, out_ref, lse_ref, *, rows, per):
    length, lanes = q_ref.shape
    lane = lax.broadcasted_iota(jnp.int32, (length, lanes), 1)
    query = (q_ref[...].astype(f32) * SCALE)
    key = k_ref[...]
    value_t = v_ref[...].astype(f32).T.astype(bf16)
    mask = causal_mask(rows)
    blocks = length // rows
    heads = [jnp.where(lane // HEAD_DIM == h, query, 0.0).astype(bf16) for h in range(per)]
    for j in range(blocks):
        cols = slice(j * rows, (j + 1) * rows)
        pieces = []
        for h in range(per):
            scores = []
            for i in range(j + 1):
                s = dot_nt(key[i * rows:(i + 1) * rows], heads[h][cols])
                scores.append(jnp.where(mask, s, -1e30) if i == j else s)
            top = scores[0].max(axis=0, keepdims=True)
            for s in scores[1:]:
                top = jnp.maximum(top, s.max(axis=0, keepdims=True))
            grown = [jnp.exp(s - top) for s in scores]
            total = grown[0].sum(axis=0, keepdims=True)
            for e in grown[1:]:
                total = total + e.sum(axis=0, keepdims=True)
            lse_ref[0, h:h + 1, cols] = top + jnp.log(total)
            inverse = 1.0 / total
            acc = None
            for i, e in enumerate(grown):
                part = dot_nn(
                    value_t[h * HEAD_DIM:(h + 1) * HEAD_DIM, i * rows:(i + 1) * rows],
                    (e * inverse).astype(bf16),
                )
                acc = part if acc is None else acc + part
            pieces.append(acc)
        out_ref[cols, :] = jnp.concatenate(pieces, axis=0).T.astype(bf16)


def attend_backward_kernel(q_ref, k_ref, v_ref, g_ref, lse_ref, out_ref, *, rows, per, width):
    at = pl.program_id(0)
    length, lanes = q_ref.shape
    lane = lax.broadcasted_iota(jnp.int32, (length, lanes), 1)
    query = q_ref[...].astype(f32) * SCALE
    grad = g_ref[...].astype(f32)
    key = k_ref[...]
    value = v_ref[...]
    key_t = key.astype(f32).T.astype(bf16)
    mask = causal_mask(rows)
    blocks = length // rows
    grad_key = [None] * blocks
    grad_value = [None] * blocks
    dq = [[None] * per for _ in range(blocks)]
    add = lambda a, b: b if a is None else a + b
    for h in range(per):
        own = lane // HEAD_DIM == h
        q_h = jnp.where(own, query, 0.0).astype(bf16)
        g_h = jnp.where(own, grad, 0.0).astype(bf16)
        for j in range(blocks):
            cols = slice(j * rows, (j + 1) * rows)
            lse = lse_ref[0, h:h + 1, cols]
            probs, drops, inner = [], [], None
            for i in range(j + 1):
                at_i = slice(i * rows, (i + 1) * rows)
                p = jnp.exp(dot_nt(key[at_i], q_h[cols]) - lse)
                if i == j:
                    p = jnp.where(mask, p, 0.0)
                d = dot_nt(value[at_i], g_h[cols])
                inner = add(inner, (p * d).sum(axis=0, keepdims=True))
                grad_value[i] = add(grad_value[i], dot_nn(p.astype(bf16), g_h[cols]))
                probs.append(p)
                drops.append(d)
            for i in range(j + 1):
                at_i = slice(i * rows, (i + 1) * rows)
                ds = (probs[i] * (drops[i] - inner)).astype(bf16)
                grad_key[i] = add(grad_key[i], dot_nn(ds, q_h[cols]))
                dq[j][h] = add(
                    dq[j][h], dot_nn(key_t[h * HEAD_DIM:(h + 1) * HEAD_DIM, at_i], ds)
                )
    for i in range(blocks):
        at_i = slice(i * rows, (i + 1) * rows)
        dq_i = jnp.concatenate(dq[i], axis=0).T * SCALE
        for slot, piece in enumerate((dq_i, grad_key[i], grad_value[i])):
            start = pl.multiple_of(slot * width + at * lanes, lanes)
            out_ref[at_i, pl.ds(start, lanes)] = piece.astype(bf16)


def attend_forward_call(packed):
    length, wide = packed.shape
    width = wide // 3
    per = LANES // HEAD_DIM
    pairs = width // LANES
    rows = length // 2
    at = lambda part: pl.BlockSpec((length, LANES), lambda h: (0, part * pairs + h))
    return pl.pallas_call(
        functools.partial(attend_forward_kernel, rows=rows, per=per),
        grid=(pairs,),
        in_specs=[at(0), at(1), at(2)],
        out_specs=[
            pl.BlockSpec((length, LANES), lambda h: (0, h)),
            pl.BlockSpec((1, per, length), lambda h: (h, 0, 0)),
        ],
        out_shape=[
            jax.ShapeDtypeStruct((length, width), bf16),
            jax.ShapeDtypeStruct((pairs, per, length), f32),
        ],
        name="attend_forward",
    )(packed, packed, packed)


def attend_backward_call(packed, grad, lse):
    length, wide = packed.shape
    width = wide // 3
    per = LANES // HEAD_DIM
    pairs = width // LANES
    rows = length // 2
    at = lambda part: pl.BlockSpec((length, LANES), lambda h: (0, part * pairs + h))
    return pl.pallas_call(
        functools.partial(attend_backward_kernel, rows=rows, per=per, width=width),
        grid=(pairs,),
        in_specs=[
            at(0), at(1), at(2),
            pl.BlockSpec((length, LANES), lambda h: (0, h)),
            pl.BlockSpec((1, per, length), lambda h: (h, 0, 0)),
        ],
        out_specs=pl.BlockSpec((length, wide), lambda h: (0, 0)),
        out_shape=jax.ShapeDtypeStruct((length, wide), bf16),
        name="attend_backward",
    )(packed, packed, packed, grad, lse)


def gelu_parts(pre):
    cdf = 0.5 * (1.0 + lax.erf(pre * (0.5 ** 0.5)))
    slope = cdf + pre * (0.3989422804014327 * jnp.exp(-0.5 * pre * pre))
    return (pre * cdf).astype(bf16), slope.astype(bf16)


def pieces_of(value, parts):
    size = value.shape[1] // parts
    return [value[:, at * size : (at + 1) * size] for at in range(parts)]


class Chain:
    def __init__(self, name, kept, sent, halves, sums, gathers):
        self.name = name
        self.halves = halves
        self.plan = [(stage, "half") for stage in halves]
        self.plan += [(stage, "sum") for stage in sums] + [(stage, "gather") for stage in gathers]
        self.gathers = gathers
        self.at = 0
        self.current = kept
        self.send(sent)

    def send(self, value):
        with jax.named_scope(f"{self.name}_{self.at}"):
            self.flight = swap(value, self.plan[self.at][0])

    def land(self):
        kind = self.plan[self.at][1]
        if kind == "gather":
            self.current = jnp.concatenate([self.current, self.flight], axis=0)
        else:
            total = self.current.astype(f32) + self.flight.astype(f32)
            self.current = total.astype(bf16)
        self.at += 1
        self.flight = None
        if self.at == len(self.plan):
            return
        kind, before = self.plan[self.at][1], self.plan[self.at - 1][1]
        if kind == "half":
            half = self.current.shape[0] // 2
            self.current, sent = self.current[:half], self.current[half:]
            self.send(sent)
            return
        if kind == "sum" or before != "gather":
            self.current = round_bf16(self.current).astype(bf16)
        if kind == "gather" and before != "gather":
            self.current = self.current[None]
        self.send(self.current)

    def finish(self):
        while self.flight is not None:
            self.land()
        if not self.gathers:
            return self.current
        count = len(self.gathers)
        natural = [stage for stage in bits_of("dp") if stage in self.gathers]
        rows = []
        for piece in range(1 << count):
            index = jnp.int32(0)
            for at, stage in enumerate(self.gathers):
                bit = (piece >> natural.index(stage)) & 1
                index = index + ((bit ^ my_bit(stage).astype(jnp.int32)) << at)
            rows.append(lax.dynamic_index_in_dim(self.current, index, 0, keepdims=False))
        return jnp.concatenate(rows, axis=0)


def bound(values, chains=(), extra=()):
    flights = [chain.flight for chain in chains]
    values, flights, extra = lax.optimization_barrier((values, flights, extra))
    for chain, flight in zip(chains, flights):
        chain.flight = flight
        chain.land()
    return (values, extra) if extra else values


def attend_forward(hidden, qkv_matrix, out_matrix, gain_row, shift_row):
    normed = layer_norm(hidden, gain_row, shift_row).astype(bf16)
    packed = jnp.dot(normed, qkv_matrix, preferred_element_type=f32).astype(bf16)
    attended, logsum = attend_forward_call(packed)
    branch = jnp.dot(attended, out_matrix, preferred_element_type=f32)
    return ((normed, packed, logsum, attended), branch)


def dot_back(grad, matrix):
    return jnp.einsum("sd,wd->sw", grad, matrix, preferred_element_type=f32)


def norm_backward(hidden, gain_row, shift_row, grad):
    ignored, pullback = jax.vjp(layer_norm, hidden, gain_row, shift_row)
    return pullback(grad)


def local(
    tokens,
    routes,
    domain_ids,
    domain_weight,
    qkv_weight,
    out_weight,
    norm_gain,
    norm_shift,
    ffn_up,
    ffn_down,
    centroid,
    expert_up,
    expert_down,
    cotangent,
):
    length, model_width = tokens.shape
    experts = centroid.shape[0]
    capacity = 5 * length // (4 * experts)
    groups = domain_weight.shape[0]
    sequences = domain_ids.shape[0]
    expert_at = lax.axis_index("expert")
    first = lax.axis_index("dp") * experts
    member = (domain_ids[:, None] == jnp.arange(groups)[None, :]).astype(f32)
    counts = jnp.sum(member, axis=0)
    weights = (
        jnp.sum(member * domain_weight, axis=1)
        * (sequences / groups)
        / jnp.sum(member * counts, axis=1)
    )
    source_weight = lax.dynamic_slice_in_dim(weights, first, experts)
    seq_weight = lax.dynamic_index_in_dim(weights, first + expert_at, 0, keepdims=False)

    route_row = routes[:, 0]
    one_hot = (route_row[:, None] == jnp.arange(experts)[None, :]).astype(jnp.int32)
    slot_ranks = jnp.sum((jnp.cumsum(one_hot, axis=0) - one_hot) * one_hot, axis=1)
    selector = one_hot.astype(bf16)
    size = capacity // PARTS
    slots = experts * size
    places = []
    for part in range(PARTS):
        local_rank = slot_ranks - part * size
        inside = (local_rank >= 0) & (local_rank < size)
        index = jnp.where(inside, route_row * size + local_rank, -1)
        places.append((jnp.arange(slots, dtype=jnp.int32)[:, None] == index[None, :]).astype(bf16))

    def exchange(table):
        table = table.reshape(experts, size, model_width)
        table = lax.all_to_all(table, "expert", split_axis=0, concat_axis=0, tiled=True)
        return table.reshape(slots, model_width)

    def to_slots(rows, part):
        return exchange(jnp.dot(places[part], rows, preferred_element_type=bf16))

    def from_slots(parts):
        total = None
        for place, back in zip(places, parts):
            rows = jnp.einsum("ps,pd->sd", place, back, preferred_element_type=f32)
            total = rows if total is None else total + rows
        return total

    cot_slots = [to_slots(cotangent, part) for part in range(PARTS)]

    hidden0 = tokens.astype(f32)
    saved0, branch0 = attend_forward(
        hidden0, qkv_weight[0], out_weight[0], norm_gain[0], norm_shift[0]
    )
    hidden1, cot_slots = bound(hidden0 + branch0, extra=tuple(cot_slots))
    fnormed = layer_norm(hidden1, norm_gain[1], norm_shift[1]).astype(bf16)
    act, slope = gelu_parts(dot_nn(fnormed, ffn_up))
    hidden2 = hidden1 + dot_nn(act, ffn_down)
    saved1, branch1 = attend_forward(
        hidden2, qkv_weight[1], out_weight[1], norm_gain[2], norm_shift[2]
    )
    hidden3 = hidden2 + branch1
    normed = layer_norm(hidden3, norm_gain[3], norm_shift[3]).astype(bf16)
    slot_in = []
    for part in range(PARTS):
        slot_in.append(to_slots(normed, part))

    up_matrix = expert_up[0]
    down_matrix = expert_down[0]
    own_centroid = lax.dynamic_index_in_dim(centroid, expert_at, 0, keepdims=True).astype(f32)
    scale = jnp.broadcast_to(source_weight[:, None], (experts, size)).reshape(slots, 1)
    eact, eout, dslot_out, grad_epre, back = [], [], [], [], []
    for part in range(PARTS):
        act_e, slope_e = gelu_parts(dot_nn(slot_in[part], up_matrix))
        out_e = dot_nn(act_e, down_matrix).astype(bf16)
        seed = cot_slots[part].astype(f32) * scale
        gate = jax.nn.sigmoid(
            jnp.sum(slot_in[part].astype(f32) * own_centroid, axis=-1, keepdims=True)
        )
        grad_out = (gate * seed).astype(bf16)
        grad_logit = jnp.sum(seed * out_e.astype(f32), axis=-1, keepdims=True)
        grad_logit = grad_logit * (gate * (1.0 - gate))
        grad_pre = (dot_back(grad_out, down_matrix) * slope_e.astype(f32)).astype(bf16)
        grad_in = dot_back(grad_pre, up_matrix) + grad_logit * own_centroid
        back.append(exchange(grad_in.astype(bf16)))
        eact.append(act_e)
        eout.append(out_e)
        dslot_out.append(grad_out)
        grad_epre.append(grad_pre)

    dp_stages = bits_of("dp")
    core = dp_stages[:1]
    chips = dp_stages[1:]
    expert_stages = bits_of("expert")
    expert_first = core + expert_stages
    dp_first = dp_stages + expert_stages
    gather_all = chips + core

    slot_in, eact, dslot_out, grad_epre = (
        jnp.concatenate(parts, axis=0) for parts in (slot_in, eact, dslot_out, grad_epre)
    )
    eup = outer_halves(slot_in, grad_epre, dp_stages)
    eact_blocks = reorder_blocks(eact, dp_stages)
    half = len(eact_blocks) // 2
    edown = [
        jnp.concatenate([outer(block, dslot_out) for block in blocks], axis=0)
        for blocks in (eact_blocks[:half], eact_blocks[half:])
    ]
    eup = Chain("eup", eup[0], eup[1], dp_stages, [], [])
    edown = Chain("edown", edown[0], edown[1], dp_stages, [], [])

    seed_grad = cotangent.astype(f32) * seq_weight
    grad_hidden, gain3, shift3 = norm_backward(
        hidden3, norm_gain[3], norm_shift[3], from_slots(back)
    )
    grad_h3 = seed_grad + grad_hidden
    grad_h3, eout = bound(grad_h3, [eup], tuple(eout))
    returned = [exchange(rows) for rows in eout]

    branch_late = grad_h3.astype(bf16)
    dattended = dot_back(branch_late, out_weight[1]).astype(bf16)
    packed_late = attend_backward_call(saved1[1], dattended, saved1[2])
    packed_late, returned = bound(packed_late, [edown], tuple(returned))
    grad_hidden, gain2, shift2 = norm_backward(
        hidden2, norm_gain[2], norm_shift[2], dot_back(packed_late, qkv_weight[1])
    )
    grad_h2 = grad_h3 + grad_hidden

    def joined(pairs, stages):
        made = [outer_halves(left, right, stages) for left, right in pairs]
        return [jnp.concatenate([one[side] for one in made], axis=1) for side in range(2)]

    late = joined([(saved1[0], packed_late), (saved1[3], branch_late)], expert_first)
    late = Chain("late", late[0], late[1], expert_first, chips, core)

    grad_h2 = bound(grad_h2)
    branch_ffn = grad_h2.astype(bf16)
    grad_pre = (dot_back(branch_ffn, ffn_down) * slope.astype(f32)).astype(bf16)
    down = outer_halves(branch_ffn, act, dp_first)
    down = Chain("down", down[0], down[1], dp_first, [], gather_all)
    grad_pre = bound(grad_pre, [late])
    grad_hidden, gain1, shift1 = norm_backward(
        hidden1, norm_gain[1], norm_shift[1], dot_back(grad_pre, ffn_up)
    )
    grad_h1 = grad_h2 + grad_hidden
    pre_blocks = jnp.stack(reorder_blocks(grad_pre, expert_stages))
    ordered = reorder_columns(fnormed, core)

    def up_outer(left):
        made = jnp.einsum("sd,esf->edf", left, pre_blocks, preferred_element_type=f32)
        return made.astype(bf16).reshape(-1, made.shape[2])

    up = [up_outer(left) for left in pieces_of(ordered, 2)]
    up = Chain("up", up[0], up[1], expert_first, chips, core)
    grad_h1 = bound(grad_h1, [down])

    branch_early = grad_h1.astype(bf16)
    dattended = dot_back(branch_early, out_weight[0]).astype(bf16)
    packed_early = attend_backward_call(saved0[1], dattended, saved0[2])
    qk_width = 2 * model_width
    qk = outer_halves(saved0[0], packed_early[:, :qk_width], dp_first)
    qk = Chain("qk", qk[0], qk[1], dp_first, [], gather_all)
    grad_hidden, gain0, shift0 = norm_backward(
        hidden0, norm_gain[0], norm_shift[0], dot_back(packed_early, qkv_weight[0])
    )
    tokens_grad = grad_h1 + grad_hidden

    chosen = jnp.dot(selector, centroid, preferred_element_type=f32)
    normed_f = normed.astype(f32)
    gate_value = jax.nn.sigmoid(jnp.sum(normed_f * chosen, axis=-1))
    picked = from_slots(returned)
    result = (hidden3 + gate_value[:, None] * picked).astype(bf16)
    grad_logit = jnp.sum(seed_grad * picked, axis=-1) * (gate_value * (1.0 - gate_value))
    centroid_part = jnp.einsum(
        "se,sd->ed",
        selector.astype(f32),
        grad_logit[:, None] * normed_f,
        precision=highest,
        preferred_element_type=f32,
    )
    small = jnp.concatenate(
        [
            jnp.stack([gain0, gain1, gain2, gain3]),
            jnp.stack([shift0, shift1, shift2, shift3]),
            centroid_part,
        ],
        axis=0,
    ).astype(bf16)
    small_rows = small.shape[0]
    small = jnp.pad(small, ((0, -small_rows % LANES), (0, 0)))
    small = reorder_columns(small, expert_first).T
    vo = joined([(saved0[0], packed_early[:, qk_width:]), (saved0[3], branch_early)], expert_first)
    vo = [
        jnp.concatenate([one, rows], axis=1) for one, rows in zip(vo, jnp.split(small, 2, axis=0))
    ]
    vo = Chain("vo", vo[0], vo[1], expert_first, chips, core)

    kept = bound((qk.current, vo.current), [late, down, up])
    qk.current, vo.current = kept
    late_rows = late.finish().astype(f32)
    expert_up_grad = eup.finish().astype(f32)[None]
    expert_down_grad = edown.finish().astype(f32)[None]
    up_rows = up.finish().astype(f32)
    down_rows = down.finish().astype(f32)
    qk_rows = qk.finish().astype(f32)
    vo_rows = vo.finish().astype(f32)
    qkv_width = 3 * model_width
    small = vo_rows[:, 2 * model_width :].T
    return (
        result,
        tokens_grad,
        jnp.stack(
            [
                jnp.concatenate([qk_rows, vo_rows[:, :model_width]], axis=1),
                late_rows[:, :qkv_width],
            ]
        ),
        jnp.stack([vo_rows[:, model_width : 2 * model_width], late_rows[:, qkv_width:]]),
        small[:4],
        small[4:8],
        up_rows,
        down_rows.T,
        small[8:small_rows],
        expert_up_grad,
        expert_down_grad,
    )


def solution(mesh):
    placed = (
        P(("dp", "expert"), None),
        P(("dp", "expert"), None),
        P(),
        P(),
        P(),
        P(),
        P(),
        P(),
        P(),
        P(),
        P(),
        P("expert", None, None),
        P("expert", None, None),
        P(("dp", "expert"), None),
    )
    return jax.shard_map(
        local,
        mesh=mesh,
        in_specs=placed,
        out_specs=(
            P(("dp", "expert"), None),
            P(("dp", "expert"), None),
            P(None, "expert", None),
            P(None, "expert", None),
            P(None, "expert"),
            P(None, "expert"),
            P(None, "expert"),
            P(None, "expert"),
            P(None, "expert"),
            P("expert", "dp", None),
            P("expert", "dp", None),
        ),
        check_vma=False,
    )
```
